32 devices in a mesh: blk: 4 (over y, x), dp: 8 (over z, core).
Axes of the slice: x: 2, y: 2, z: 4, core: 2. Of those that a mesh axis runs over, the one named last changes fastest.
Arguments:
- embed: bfloat16 [8192, 768], P(('blk', 'dp')), may hold values from -0.23925781 to 0.23925781
- log_scale: float32 [1], replicated, may hold values from 3 to 3.7
- bias: float32 [1], replicated, may hold values from -5.5 to -3.5
- partner_count: int32 [8192], P(('blk', 'dp')), may hold values from 1 to 4, as said below
- partner_owner: int32 [8192, 4], P(('blk', 'dp')), may hold values from 0 to 31, as said below
- partner_row: int32 [8192, 4], P(('blk', 'dp')), may hold values from 0 to 255
Outputs:
- embed_grad: bfloat16 [8192, 768], P(('blk', 'dp'))
The draws below stay inside these ranges and needn't reach their ends.
Inputs may be any that keep to these rules, and one draw needn't show every extreme that they name: `partner_count`: 4 on some row of every device. `partner_owner`: every entry names a device other than the row's own device (devices numbered index along blk times 8 plus index along dp). Among the first partner_count entries of the rows of one device, no device is named more than 34 times, and some device exactly 34 times.
All inputs are finite; a program needn't handle non-finite values.
Results may differ from the reference program's by a relative error of at most 0.0065.
Values may be sent and summed in bfloat16 or wider, within the bound.
A program may use at most 64 MiB of HBM per device.

```python
import math
import jax
import jax.numpy as jnp
from jax import lax

D = 768
ROWS_DEV = 256
KMAX = 4
ROWS = 8192
GROUP = 1024
CAP = 34
N_BLK = 4
N_DP = 8
DEVICES = 32


def partner_tables(key):
    valid_owners = DEVICES - 1

    def one_device(dev_key, device):
        keys = jax.random.split(dev_key, 5)
        level = jax.random.randint(keys[0], (), 1, KMAX + 1)
        counts = jax.random.randint(keys[1], (ROWS_DEV,), 0, KMAX + 1) % (KMAX + 1 - level) + level
        forced = jax.random.randint(keys[2], (), 0, ROWS_DEV)
        counts = jnp.where(jnp.arange(ROWS_DEV) == forced, KMAX, counts).astype(jnp.int32)
        hot = jax.random.randint(keys[3], (), 0, valid_owners)
        others = jnp.arange((valid_owners - 1) * CAP, dtype=jnp.int32) // CAP
        others = others + (others >= hot).astype(jnp.int32)
        others = jax.random.permutation(keys[4], others)
        sequence = jnp.concatenate([jnp.full((CAP,), hot, jnp.int32), others])
        starts = jnp.cumsum(counts) - counts
        positions = starts[:, None] + jnp.arange(KMAX, dtype=jnp.int32)[None, :]
        positions = jnp.minimum(positions, valid_owners * CAP - 1)
        chosen = sequence[positions]
        owners = chosen + (chosen >= device).astype(jnp.int32)
        return (counts, owners.astype(jnp.int32))
    dev_keys = jax.random.split(jax.random.fold_in(key, 17), DEVICES)
    counts, owners = jax.vmap(one_device)(dev_keys, jnp.arange(DEVICES, dtype=jnp.int32))
    return (counts.reshape(ROWS), owners.reshape(ROWS, KMAX))


def draw_partner_count(key, part):
    return partner_tables(key)[0]


def draw_partner_owner(key, part):
    return partner_tables(key)[1]


def with_ends(values, stream_key, low, high):
    spot = [jax.random.randint(jax.random.fold_in(stream_key, axis), (), 0, length) for axis, length in enumerate(values.shape)]
    main_axis = values.shape.index(max(values.shape))
    next_to = spot[:main_axis] + [(spot[main_axis] + 1) % values.shape[main_axis]] + spot[main_axis + 1:]
    return values.at[tuple(spot)].set(low).at[tuple(next_to)].set(high)


def steps_of(rng, shape, shards, smallest, high):
    gain = 1.0
    for position, shards_of in shards:
        heights = jax.random.uniform(jax.random.fold_in(jax.random.fold_in(rng, 6), position), (shards_of,), jnp.float32, smallest / len(shards), high / len(shards))
        gain = gain * jnp.repeat(jnp.exp(heights), shape[position] // shards_of).reshape((-1,) + (1,) * (len(shape) - 1 - position))
    return gain


def scatter_about(key, extent, deviation, reach, shards=(), kind=jnp.bfloat16):
    array = jax.random.normal(key, extent, jnp.float32) * deviation
    if len(shards) > 0:
        array = steps_of(key, extent, shards, -0.22, 0.18) * array
    return jnp.clip(array, min=-reach, max=reach).astype(kind)


def setup_inputs(seed: int = 0) -> dict:
    splits = jax.random.split(jax.random.key(seed), 7)
    embed = scatter_about(splits[0], (ROWS, D), 0.04, 0.23925781, ((0, 32),))
    log_scale = jnp.clip(jax.random.uniform(splits[1], (1,), jnp.float32, 3.0, 3.7), 3.0, 3.7)
    bias = jnp.clip(jax.random.uniform(splits[2], (1,), jnp.float32, -5.5, -3.5), -5.5, -3.5)
    partner_count = draw_partner_count(jax.random.fold_in(splits[6], 71), 0)
    partner_owner = draw_partner_owner(jax.random.fold_in(splits[6], 71), 0)
    partner_row = with_ends(jax.random.randint(splits[5], (ROWS, KMAX), 0, ROWS_DEV), jax.random.fold_in(splits[5], 1), 0, ROWS_DEV - 1).astype(jnp.int32)
    return dict(embed=embed, log_scale=log_scale, bias=bias, partner_count=partner_count, partner_owner=partner_owner, partner_row=partner_row)


def reference(embed, log_scale, bias, partner_count, partner_owner, partner_row):
    highest = lax.Precision.HIGHEST
    values = embed.astype(jnp.float32)
    inv_norm = lax.rsqrt(lax.optimization_barrier(jnp.mean(values * values, axis=1, keepdims=True)) + 1e-06)
    root_width = 1.0 / math.sqrt(D)
    unit_rows = (values * inv_norm * root_width).astype(jnp.bfloat16)
    logit_scale = jnp.exp(log_scale[0])
    logit_bias = bias[0]
    blocks = unit_rows.reshape(N_BLK, N_DP, ROWS_DEV, D)

    def negative(device):
        cycle_pos = device // N_DP
        group_id = device % N_DP
        group = lax.dynamic_index_in_dim(blocks, group_id, 1, keepdims=False).reshape(GROUP, D).astype(jnp.float32)
        own_rows = lax.dynamic_slice_in_dim(group, cycle_pos * ROWS_DEV, ROWS_DEV, 0)
        scores = jnp.dot(own_rows, group.T, precision=highest)
        here = cycle_pos * ROWS_DEV + jnp.arange(ROWS_DEV, dtype=jnp.int32)
        columns = jnp.arange(GROUP, dtype=jnp.int32)
        weights = jnp.where(here[:, None] == columns[None, :], jnp.float32(0.0), jax.nn.sigmoid(logit_bias + logit_scale * scores))
        weights = weights.astype(jnp.bfloat16).astype(jnp.float32)
        return 2.0 * logit_scale * jnp.dot(weights, group, precision=highest)
    neg_grad = lax.map(negative, jnp.arange(DEVICES, dtype=jnp.int32)).reshape(ROWS, D)
    global_index = (partner_owner * ROWS_DEV + partner_row).astype(jnp.int32)
    live_all = jnp.arange(KMAX, dtype=jnp.int32)[None, :] < partner_count[:, None]

    def positive(incoming, device):
        start = (device * ROWS_DEV).astype(jnp.int32)
        own_rows = lax.dynamic_slice_in_dim(unit_rows, start, ROWS_DEV, 0).astype(jnp.float32)
        index = lax.dynamic_slice_in_dim(global_index, start, ROWS_DEV, 0)
        live = lax.dynamic_slice_in_dim(live_all, start, ROWS_DEV, 0)
        partner = unit_rows[index.reshape(-1)].astype(jnp.float32).reshape(ROWS_DEV, KMAX, D)
        scores = jnp.einsum('rd,rkd->rk', own_rows, partner, precision=highest)
        weight = jnp.where(live, jax.nn.sigmoid(-(logit_bias + logit_scale * scores)), jnp.float32(0.0))
        own_term = (-logit_scale * weight[:, :, None] * partner).astype(jnp.bfloat16)
        back_term = (-logit_scale * weight[:, :, None] * own_rows[:, None, :]).astype(jnp.bfloat16)
        incoming = incoming.at[index.reshape(-1)].add(back_term.reshape(-1, D).astype(jnp.float32))
        return (incoming, lax.optimization_barrier(jnp.sum(own_term.astype(jnp.float32), axis=1)))
    incoming, own_sum = lax.scan(positive, jnp.zeros((ROWS, D), jnp.float32), jnp.arange(DEVICES, dtype=jnp.int32))
    row_grad = neg_grad + own_sum.reshape(ROWS, D) + incoming
    inner = lax.optimization_barrier(jnp.sum(values * row_grad, axis=1, keepdims=True))
    result = root_width * inv_norm * (row_grad - values * inv_norm * inv_norm * inner / D)
    return result.astype(jnp.bfloat16)
```

```python
import functools
import math

import jax
import jax.numpy as jnp
from jax import lax
from jax.experimental import pallas as pl
from jax.experimental.pallas import tpu as pltpu
from jax.sharding import PartitionSpec as P

MESH = pl.DeviceIdType.MESH


def lookup(table, index):
    value = jnp.int32(table[0])
    for k in range(1, len(table)):
        value = jnp.where(index == k, jnp.int32(table[k]), value)
    return value


def kernel(
    n_blk, n_dp, log_scale_ref, bias_ref, x_ref, mine_ref, theirs_ref, o_ref,
    buf, keys, acc, wanted, z_sem, right_sem, left_sem, sib_sem, recv_sem, key_send, key_recv,
):
    rows, width = x_ref.shape
    most = mine_ref.shape[1]
    half = rows // 2
    n_all = n_blk * n_dp
    n_z = n_dp // 2
    far = n_blk // 2
    events = n_blk * n_z
    i, j = lax.axis_index("blk"), lax.axis_index("dp")
    z, c = j // 2, j % 2
    me = i * n_dp + j

    ring = [p ^ (p >> 1) for p in range(n_blk)]
    place = [ring.index(k) for k in range(n_blk)]
    pos = lookup(place, i)
    blk_at = lambda p: lookup(ring, lax.rem(p + n_blk, n_blk))
    right, left = blk_at(pos + 1), blk_at(pos - 1)
    order = []
    for a in range(n_z):
        order += sorted(range(n_z), key=lambda b: (abs(b - a), b))
    z_at = lambda t: lookup(order, z * n_z + t)
    slot = lambda bi, zz, cc: (bi * n_z + zz) * 2 + cc

    def copy(f, h, device, send, recv):
        if h is None:
            span = pl.ds(pl.multiple_of(f * rows, rows), rows)
        else:
            span = pl.ds(pl.multiple_of(f * rows + h * half, half), half)
        return pltpu.make_async_remote_copy(
            src_ref=buf.at[span], dst_ref=buf.at[span], send_sem=send, recv_sem=recv,
            device_id=device, device_id_type=MESH,
        )

    def to_right(f, h, e):
        return copy(f, h, (right, j), right_sem.at[e], recv_sem.at[f, h or 0])

    def to_left(f, h, e):
        return copy(f, h, (left, j), left_sem.at[e], recv_sem.at[f, h or 0])

    def to_sib(f, e):
        return copy(f, None, (i, z * 2 + 1 - c), sib_sem.at[e], recv_sem.at[f, 0])

    def to_z(t):
        return copy(me, None, (i, z_at(t) * 2 + c), z_sem.at[t], recv_sem.at[me, 0])

    def arrived(f, h):
        copy(f, h, (right, j), right_sem.at[0], recv_sem.at[f, h or 0]).wait_recv()

    def place_of(e):
        t, m = e // n_blk, e % n_blk
        d = (m + 1) // 2
        return t, m, d, blk_at(jnp.where(m % 2 == 1, pos - d, pos + d)), z_at(t)

    barrier = pltpu.get_barrier_semaphore()

    @pl.loop(1, n_all)
    def _(k):
        f = lax.rem(me + k, n_all)
        pl.semaphore_signal(barrier, 1, device_id=(f // n_dp, f % n_dp), device_id_type=MESH)

    root = 1.0 / math.sqrt(width)
    x = x_ref[...].astype(jnp.float32)
    inv = lax.rsqrt(jnp.mean(x * x, axis=1, keepdims=True) + 1e-06)
    own = pl.ds(pl.multiple_of(me * rows, rows), rows)
    buf[own, :] = (x * inv * root).astype(jnp.bfloat16)
    keys[pl.ds(me, 1)] = theirs_ref[...]
    pl.semaphore_wait(barrier, n_all - 1)

    to_right(me, None, 0).start()
    to_left(me, None, 0).start()
    for t in range(1, n_z):
        to_z(t).start()
    to_sib(me, 0).start()

    def key_copy(src, dst, f):
        return pltpu.make_async_remote_copy(
            src_ref=src, dst_ref=dst, send_sem=key_send, recv_sem=key_recv,
            device_id=(f // n_dp, f % n_dp), device_id_type=MESH,
        )

    @pl.loop(1, n_all)
    def _(k):
        f = lax.rem(me + k, n_all)
        key_copy(theirs_ref, keys.at[pl.ds(me, 1)], f).start()

    acc[...] = jnp.zeros_like(acc)
    for k in range(most):
        wanted[k] = jnp.broadcast_to(mine_ref[:, k : k + 1], (rows, 128))
    scale = jnp.exp(jnp.full((1, 1), log_scale_ref[0], jnp.float32))
    offset = jnp.full((1, 1), bias_ref[0], jnp.float32)
    everything = keys.at[pl.ds(0, n_all - 1)]
    key_copy(everything, everything, lax.rem(me + 1, n_all)).wait()

    def compute(e):
        _, _, _, bi, zz = place_of(e)
        arrived(slot(bi, zz, 1 - c), None)
        pair = bi * n_z + zz
        start = pair * 2 * rows
        block = buf[pl.ds(pl.multiple_of(start, 2 * rows), 2 * rows), :]
        scores = lax.dot_general(
            buf[own, :], block, (((1,), (1,)), ((), ())), preferred_element_type=jnp.float32
        )
        lanes = lax.broadcasted_iota(jnp.int32, (rows, 128), 1)
        here = lax.broadcasted_iota(jnp.int32, (rows, 128), 0) + me * rows
        weights = []
        for u in range(2 * rows // 128):
            side, at = u * 128 // rows, u * 128 % rows
            columns = lanes + (start + u * 128)
            named = jnp.zeros((rows, 128), jnp.float32)
            for k in range(most):
                named += jnp.where(wanted[k] == columns, 1.0, 0.0)
            for k in range(most):
                key = keys[pair * 2 + side, k : k + 1, at : at + 128]
                named += jnp.where(key == here, 1.0, 0.0)
            power = jnp.exp(offset + scale * scores[:, u * 128 : (u + 1) * 128])
            gain = jnp.where(jnp.logical_and(zz == z, c == side), 2.0, 0.0)
            negative = jnp.where(columns == here, 0.0, gain * power)
            weights.append(((negative - named) / (1.0 + power)).astype(jnp.bfloat16))
        weight = jnp.concatenate(weights, axis=1)
        acc[...] += jnp.dot(weight, block, preferred_element_type=jnp.float32)

    @pl.loop(0, events)
    def _(e):
        t, m, d, bi, zz = place_of(e)

        @pl.when(jnp.logical_and(m == 0, t + 1 < n_z))
        def _():
            f = slot(i, z_at(t + 1), c)
            arrived(f, None)
            to_right(f, None, e + n_blk).start()
            to_left(f, None, e + n_blk).start()
            to_sib(f, e + n_blk).start()

        f = slot(bi, zz, c)

        @pl.when(jnp.logical_and(m > 0, m < n_blk - 1))
        def _():
            arrived(f, None)

        for parity, send in ((1, to_right), (0, to_left)):
            mine = jnp.logical_and(jnp.logical_and(m > 0, m < n_blk - 1), m % 2 == parity)

            @pl.when(jnp.logical_and(mine, d == far - 1))
            def _():
                send(f, 1 - parity, e).start()

            if far > 2:
                @pl.when(jnp.logical_and(mine, d < far - 1))
                def _():
                    send(f, None, e).start()

        @pl.when(m == n_blk - 1)
        def _():
            arrived(f, 0)
            arrived(f, 1)

        @pl.when(m > 0)
        def _():
            to_sib(f, e).start()

        @pl.when(e > 0)
        def _():
            compute(e - 1)

    compute(events - 1)

    t_acc = scale * acc[...]
    x = x_ref[...].astype(jnp.float32)
    inv = lax.rsqrt(jnp.mean(x * x, axis=1, keepdims=True) + 1e-06)
    inner = jnp.sum(x * t_acc, axis=1, keepdims=True)
    o_ref[...] = (root * inv * (t_acc - x * (inv * inv * inner / width))).astype(o_ref.dtype)

    for t in range(1, n_z):
        to_z(t).wait_send()

    @pl.loop(0, events)
    def _(e):
        t, m, d, bi, zz = place_of(e)
        f = slot(bi, zz, c)
        to_sib(f, e).wait_send()

        @pl.when(m == 0)
        def _():
            to_right(f, None, e).wait_send()
            to_left(f, None, e).wait_send()

        for parity, send in ((1, to_right), (0, to_left)):
            mine = jnp.logical_and(jnp.logical_and(m > 0, m < n_blk - 1), m % 2 == parity)

            @pl.when(jnp.logical_and(mine, d == far - 1))
            def _():
                send(f, 1 - parity, e).wait_send()

            if far > 2:
                @pl.when(jnp.logical_and(mine, d < far - 1))
                def _():
                    send(f, None, e).wait_send()


def body(n_blk, n_dp, embed, log_scale, bias, partner_count, partner_owner, partner_row):
    rows, width = embed.shape
    most = partner_owner.shape[1]
    n_all = n_blk * n_dp
    events = n_all // 2
    live = jnp.arange(most, dtype=jnp.int32)[None, :] < partner_count[:, None]
    mine = jnp.where(live, partner_owner * rows + partner_row, -1)
    theirs = mine.T.reshape(1, most, rows)
    vmem = pl.BlockSpec(memory_space=pltpu.VMEM)
    smem = pl.BlockSpec(memory_space=pltpu.SMEM)
    return pl.pallas_call(
        functools.partial(kernel, n_blk, n_dp),
        out_shape=jax.ShapeDtypeStruct((rows, width), embed.dtype),
        in_specs=[smem, smem, vmem, vmem, vmem],
        out_specs=vmem,
        scratch_shapes=[
            pltpu.VMEM((n_all * rows, width), jnp.bfloat16),
            pltpu.VMEM((n_all, most, rows), jnp.int32),
            pltpu.VMEM((rows, width), jnp.float32),
            pltpu.VMEM((most, rows, 128), jnp.int32),
            pltpu.SemaphoreType.DMA((n_dp // 2,)),
            pltpu.SemaphoreType.DMA((events,)),
            pltpu.SemaphoreType.DMA((events,)),
            pltpu.SemaphoreType.DMA((events,)),
            pltpu.SemaphoreType.DMA((n_all, 2)),
            pltpu.SemaphoreType.DMA,
            pltpu.SemaphoreType.DMA,
        ],
        compiler_params=pltpu.CompilerParams(
            collective_id=0, has_side_effects=True, vmem_limit_bytes=60 * 1024 * 1024
        ),
    )(log_scale, bias, embed, mine, theirs)


def solution(mesh):
    return jax.shard_map(
        functools.partial(body, mesh.shape["blk"], mesh.shape["dp"]),
        mesh=mesh,
        in_specs=(
            P(("blk", "dp"), None),
            P(),
            P(),
            P(("blk", "dp")),
            P(("blk", "dp"), None),
            P(("blk", "dp"), None),
        ),
        out_specs=P(("blk", "dp"), None),
        check_vma=False,
    )
```

```python
import functools
import math

import jax
import jax.numpy as jnp
from jax import lax
from jax.experimental import pallas as pl
from jax.experimental.pallas import tpu as pltpu
from jax.sharding import PartitionSpec as P

MESH = pl.DeviceIdType.MESH


def lookup(table, index):
    value = jnp.int32(table[0])
    for k in range(1, len(table)):
        value = jnp.where(index == k, jnp.int32(table[k]), value)
    return value


def kernel(
    n_blk, n_dp, log_scale_ref, bias_ref, x_ref, mine_ref, theirs_ref, o_ref,
    buf, keys, acc, wanted, z_sem, right_sem, left_sem, sib_sem, recv_sem, key_send, key_recv,
):
    rows, width = x_ref.shape
    most = mine_ref.shape[1]
    half = rows // 2
    n_all = n_blk * n_dp
    n_z = n_dp // 2
    far = n_blk // 2
    events = n_blk * n_z
    i, j = lax.axis_index("blk"), lax.axis_index("dp")
    z, c = j // 2, j % 2
    me = i * n_dp + j

    ring = [p ^ (p >> 1) for p in range(n_blk)]
    place = [ring.index(k) for k in range(n_blk)]
    pos = lookup(place, i)
    blk_at = lambda p: lookup(ring, lax.rem(p + n_blk, n_blk))
    right, left = blk_at(pos + 1), blk_at(pos - 1)
    order = []
    for a in range(n_z):
        order += sorted(range(n_z), key=lambda b: (abs(b - a), b))
    z_at = lambda t: lookup(order, z * n_z + t)
    slot = lambda bi, zz, cc: (bi * n_z + zz) * 2 + cc

    def copy(f, h, device, send, recv):
        if h is None:
            span = pl.ds(pl.multiple_of(f * rows, rows), rows)
        else:
            span = pl.ds(pl.multiple_of(f * rows + h * half, half), half)
        return pltpu.make_async_remote_copy(
            src_ref=buf.at[span], dst_ref=buf.at[span], send_sem=send, recv_sem=recv,
            device_id=device, device_id_type=MESH,
        )

    def to_right(f, h, e):
        return copy(f, h, (right, j), right_sem.at[e], recv_sem.at[f, h or 0])

    def to_left(f, h, e):
        return copy(f, h, (left, j), left_sem.at[e], recv_sem.at[f, h or 0])

    def to_sib(f, e):
        return copy(f, None, (i, z * 2 + 1 - c), sib_sem.at[e], recv_sem.at[f, 0])

    def along_z(zz, step, k):
        f = slot(i, zz, c)
        return copy(f, None, (i, (z + step) * 2 + c), z_sem.at[zz, k], recv_sem.at[f, 0])

    def arrived(f, h):
        copy(f, h, (right, j), right_sem.at[0], recv_sem.at[f, h or 0]).wait_recv()

    def place_of(e):
        t, m = e // n_blk, e % n_blk
        t = jnp.where(m == n_blk - 1, t - 1, t)
        d = (m + 1) // 2
        return t, m, d, blk_at(jnp.where(m % 2 == 1, pos - d, pos + d)), z_at(t)

    barrier = pltpu.get_barrier_semaphore()

    @pl.loop(1, n_all)
    def _(k):
        f = lax.rem(me + k, n_all)
        pl.semaphore_signal(barrier, 1, device_id=(f // n_dp, f % n_dp), device_id_type=MESH)

    root = 1.0 / math.sqrt(width)
    x = x_ref[...].astype(jnp.float32)
    inv = lax.rsqrt(jnp.mean(x * x, axis=1, keepdims=True) + 1e-06)
    own = pl.ds(pl.multiple_of(me * rows, rows), rows)
    buf[own, :] = (x * inv * root).astype(jnp.bfloat16)
    keys[pl.ds(me, 1)] = theirs_ref[...]
    pl.semaphore_wait(barrier, n_all - 1)

    to_right(me, None, z).start()
    to_left(me, None, z).start()

    @pl.when(z < n_z - 1)
    def _():
        along_z(z, 1, 0).start()

    @pl.when(z > 0)
    def _():
        along_z(z, -1, 1).start()

    to_sib(me, z).start()

    def key_copy(src, dst, f):
        return pltpu.make_async_remote_copy(
            src_ref=src, dst_ref=dst, send_sem=key_send, recv_sem=key_recv,
            device_id=(f // n_dp, f % n_dp), device_id_type=MESH,
        )

    @pl.loop(1, n_all)
    def _(k):
        f = lax.rem(me + k, n_all)
        key_copy(theirs_ref, keys.at[pl.ds(me, 1)], f).start()

    acc[...] = jnp.zeros_like(acc)
    for k in range(most):
        wanted[k] = jnp.broadcast_to(mine_ref[:, k : k + 1], (rows, 128))
    scale = jnp.exp(jnp.full((1, 1), log_scale_ref[0], jnp.float32))
    offset = jnp.full((1, 1), bias_ref[0], jnp.float32)
    everything = keys.at[pl.ds(0, n_all - 1)]
    key_copy(everything, everything, lax.rem(me + 1, n_all)).wait()

    def compute(e):
        _, _, _, bi, zz = place_of(e)
        arrived(slot(bi, zz, 1 - c), None)
        pair = bi * n_z + zz
        start = pair * 2 * rows
        block = buf[pl.ds(pl.multiple_of(start, 2 * rows), 2 * rows), :]
        scores = lax.dot_general(
            buf[own, :], block, (((1,), (1,)), ((), ())), preferred_element_type=jnp.float32
        )
        lanes = lax.broadcasted_iota(jnp.int32, (rows, 128), 1)
        here = lax.broadcasted_iota(jnp.int32, (rows, 128), 0) + me * rows
        weights = []
        for u in range(2 * rows // 128):
            side, at = u * 128 // rows, u * 128 % rows
            columns = lanes + (start + u * 128)
            named = jnp.zeros((rows, 128), jnp.float32)
            for k in range(most):
                named += jnp.where(wanted[k] == columns, 1.0, 0.0)
            for k in range(most):
                key = keys[pair * 2 + side, k : k + 1, at : at + 128]
                named += jnp.where(key == here, 1.0, 0.0)
            power = jnp.exp(offset + scale * scores[:, u * 128 : (u + 1) * 128])
            gain = jnp.where(jnp.logical_and(zz == z, c == side), 2.0, 0.0)
            negative = jnp.where(columns == here, 0.0, gain * power)
            weights.append(((negative - named) / (1.0 + power)).astype(jnp.bfloat16))
        weight = jnp.concatenate(weights, axis=1)
        acc[...] += jnp.dot(weight, block, preferred_element_type=jnp.float32)

    @pl.loop(0, events + n_blk)
    def _(e):
        t, m, d, bi, zz = place_of(e)
        valid = jnp.logical_and(t >= 0, t < n_z)

        for step, k in ((1, 1), (-1, 0)):
            origin = z + step * (t + 1)

            @pl.when(jnp.logical_and(m == 0, jnp.logical_and(origin >= 0, origin < n_z)))
            def _():
                f = slot(i, origin, c)
                arrived(f, None)

                @pl.when(jnp.logical_and(z - step >= 0, z - step < n_z))
                def _():
                    along_z(origin, -step, k).start()

                to_right(f, None, origin).start()
                to_left(f, None, origin).start()
                to_sib(f, origin).start()

        f = slot(bi, zz, c)
        passing = jnp.logical_and(valid, jnp.logical_and(m > 0, m < n_blk - 1))

        @pl.when(passing)
        def _():
            arrived(f, None)

        for parity, send in ((1, to_right), (0, to_left)):
            mine = jnp.logical_and(passing, m % 2 == parity)

            @pl.when(jnp.logical_and(mine, d == far - 1))
            def _():
                send(f, 1 - parity, m * n_z + zz).start()

            if far > 2:
                @pl.when(jnp.logical_and(mine, d < far - 1))
                def _():
                    send(f, None, m * n_z + zz).start()

        @pl.when(jnp.logical_and(valid, m == n_blk - 1))
        def _():
            arrived(f, 0)
            arrived(f, 1)

        @pl.when(jnp.logical_and(valid, m > 0))
        def _():
            to_sib(f, m * n_z + zz).start()

        before = place_of(e - 1 + n_blk)[0] - 1

        @pl.when(jnp.logical_and(e > 0, jnp.logical_and(before >= 0, before < n_z)))
        def _():
            compute(e - 1)

    compute(events + n_blk - 1)

    t_acc = scale * acc[...]
    x = x_ref[...].astype(jnp.float32)
    inv = lax.rsqrt(jnp.mean(x * x, axis=1, keepdims=True) + 1e-06)
    inner = jnp.sum(x * t_acc, axis=1, keepdims=True)
    o_ref[...] = (root * inv * (t_acc - x * (inv * inv * inner / width))).astype(o_ref.dtype)

    @pl.loop(0, n_z)
    def _(zz):
        @pl.when(jnp.logical_and(zz <= z, z < n_z - 1))
        def _():
            along_z(zz, 1, 0).wait_send()

        @pl.when(jnp.logical_and(zz >= z, z > 0))
        def _():
            along_z(zz, -1, 1).wait_send()

    @pl.loop(0, events)
    def _(e):
        m, zz = e // n_z, e % n_z
        to_sib(me, e).wait_send()

        @pl.when(m == 0)
        def _():
            to_right(me, None, e).wait_send()
            to_left(me, None, e).wait_send()

        passing = jnp.logical_and(m > 0, m < n_blk - 1)
        for parity, send in ((1, to_right), (0, to_left)):
            mine = jnp.logical_and(passing, m % 2 == parity)

            @pl.when(jnp.logical_and(mine, (m + 1) // 2 == far - 1))
            def _():
                send(me, 0, e).wait_send()

            if far > 2:
                @pl.when(jnp.logical_and(mine, (m + 1) // 2 < far - 1))
                def _():
                    send(me, None, e).wait_send()


def body(n_blk, n_dp, embed, log_scale, bias, partner_count, partner_owner, partner_row):
    rows, width = embed.shape
    most = partner_owner.shape[1]
    n_all = n_blk * n_dp
    events = n_all // 2
    live = jnp.arange(most, dtype=jnp.int32)[None, :] < partner_count[:, None]
    mine = jnp.where(live, partner_owner * rows + partner_row, -1)
    theirs = mine.T.reshape(1, most, rows)
    vmem = pl.BlockSpec(memory_space=pltpu.VMEM)
    smem = pl.BlockSpec(memory_space=pltpu.SMEM)
    return pl.pallas_call(
        functools.partial(kernel, n_blk, n_dp),
        out_shape=jax.ShapeDtypeStruct((rows, width), embed.dtype),
        in_specs=[smem, smem, vmem, vmem, vmem],
        out_specs=vmem,
        scratch_shapes=[
            pltpu.VMEM((n_all * rows, width), jnp.bfloat16),
            pltpu.VMEM((n_all, most, rows), jnp.int32),
            pltpu.VMEM((rows, width), jnp.float32),
            pltpu.VMEM((most, rows, 128), jnp.int32),
            pltpu.SemaphoreType.DMA((n_dp // 2, 2)),
            pltpu.SemaphoreType.DMA((events,)),
            pltpu.SemaphoreType.DMA((events,)),
            pltpu.SemaphoreType.DMA((events,)),
            pltpu.SemaphoreType.DMA((n_all, 2)),
            pltpu.SemaphoreType.DMA,
            pltpu.SemaphoreType.DMA,
        ],
        compiler_params=pltpu.CompilerParams(
            collective_id=0, has_side_effects=True, vmem_limit_bytes=60 * 1024 * 1024
        ),
    )(log_scale, bias, embed, mine, theirs)


def solution(mesh):
    return jax.shard_map(
        functools.partial(body, mesh.shape["blk"], mesh.shape["dp"]),
        mesh=mesh,
        in_specs=(
            P(("blk", "dp"), None),
            P(),
            P(),
            P(("blk", "dp")),
            P(("blk", "dp"), None),
            P(("blk", "dp"), None),
        ),
        out_specs=P(("blk", "dp"), None),
        check_vma=False,
    )
```

```python
import functools
import math

import jax
import jax.numpy as jnp
from jax import lax
from jax.experimental import pallas as pl
from jax.experimental.pallas import tpu as pltpu
from jax.sharding import PartitionSpec as P

MESH = pl.DeviceIdType.MESH


def lookup(table, index):
    value = jnp.int32(table[0])
    for k in range(1, len(table)):
        value = jnp.where(index == k, jnp.int32(table[k]), value)
    return value


def kernel(
    n_blk, n_dp, log_scale_ref, bias_ref, x_ref, theirs_ref, o_ref,
    buf, keys, acc, wanted, z_sem, right_sem, left_sem, sib_sem, recv_sem, key_send, key_recv,
):
    rows, width = x_ref.shape
    most = theirs_ref.shape[1]
    half = rows // 2
    n_all = n_blk * n_dp
    n_z = n_dp // 2
    far = n_blk // 2
    events = n_blk * n_z
    i, j = lax.axis_index("blk"), lax.axis_index("dp")
    z, c = j // 2, j % 2
    me = i * n_dp + j

    ring = [p ^ (p >> 1) for p in range(n_blk)]
    place = [ring.index(k) for k in range(n_blk)]
    pos = lookup(place, i)
    blk_at = lambda p: lookup(ring, lax.rem(p + n_blk, n_blk))
    right, left = blk_at(pos + 1), blk_at(pos - 1)
    order = []
    for a in range(n_z):
        order += sorted(range(n_z), key=lambda b: (abs(b - a), b))
    z_at = lambda t: lookup(order, z * n_z + t)
    slot = lambda bi, zz, cc: (bi * n_z + zz) * 2 + cc

    def copy(f, h, device, send, recv):
        if h is None:
            span = pl.ds(pl.multiple_of(f * rows, rows), rows)
        else:
            span = pl.ds(pl.multiple_of(f * rows + h * half, half), half)
        return pltpu.make_async_remote_copy(
            src_ref=buf.at[span], dst_ref=buf.at[span], send_sem=send, recv_sem=recv,
            device_id=device, device_id_type=MESH,
        )

    def to_right(f, h, e):
        return copy(f, h, (right, j), right_sem.at[e], recv_sem.at[f, h or 0])

    def to_left(f, h, e):
        return copy(f, h, (left, j), left_sem.at[e], recv_sem.at[f, h or 0])

    def to_sib(f, e):
        return copy(f, None, (i, z * 2 + 1 - c), sib_sem.at[e], recv_sem.at[f, 0])

    def along_z(zz, step, k):
        f = slot(i, zz, c)
        return copy(f, None, (i, (z + step) * 2 + c), z_sem.at[zz, k], recv_sem.at[f, 0])

    far_blk = blk_at(pos + far)

    def far_along_z(zz, step, k):
        f = slot(far_blk, zz, c)
        return copy(f, None, (i, (z + step) * 2 + c), z_sem.at[zz, 2 + k], recv_sem.at[f, 0])

    def reach(zz):
        return jnp.where(jnp.logical_and(zz >= 0, zz < n_z), 1, 0)

    def halves(zz):
        return jnp.logical_or(zz == z, jnp.maximum(zz - z, z - zz) > reach(z))

    def arrived(f, h):
        copy(f, h, (right, j), right_sem.at[0], recv_sem.at[f, h or 0]).wait_recv()

    def place_of(e):
        t, m = e // n_blk, e % n_blk
        t = jnp.where(m == n_blk - 1, t - 1, t)
        d = (m + 1) // 2
        return t, m, d, blk_at(jnp.where(m % 2 == 1, pos - d, pos + d)), z_at(t)

    barrier = pltpu.get_barrier_semaphore()

    @pl.loop(1, n_all)
    def _(k):
        f = lax.rem(me + k, n_all)
        pl.semaphore_signal(barrier, 1, device_id=(f // n_dp, f % n_dp), device_id_type=MESH)

    root = 1.0 / math.sqrt(width)
    x = x_ref[...].astype(jnp.float32)
    inv = lax.rsqrt(jnp.mean(x * x, axis=1, keepdims=True) + 1e-06)
    own = pl.ds(pl.multiple_of(me * rows, rows), rows)
    buf[own, :] = (x * inv * root).astype(jnp.bfloat16)
    keys[pl.ds(me, 1)] = theirs_ref[...]
    pl.semaphore_wait(barrier, n_all - 1)

    to_right(me, None, z).start()
    to_left(me, None, z).start()

    @pl.when(z < n_z - 1)
    def _():
        along_z(z, 1, 0).start()

    @pl.when(z > 0)
    def _():
        along_z(z, -1, 1).start()

    to_sib(me, z).start()

    def key_copy(src, dst, f):
        return pltpu.make_async_remote_copy(
            src_ref=src, dst_ref=dst, send_sem=key_send, recv_sem=key_recv,
            device_id=(f // n_dp, f % n_dp), device_id_type=MESH,
        )

    @pl.loop(1, n_all)
    def _(k):
        f = lax.rem(me + k, n_all)
        key_copy(theirs_ref, keys.at[pl.ds(me, 1)], f).start()

    acc[...] = jnp.zeros_like(acc)
    for k in range(most):
        wanted[k] = jnp.broadcast_to(theirs_ref[0, k : k + 1, :], (128, rows)).T
    scale = jnp.exp(jnp.full((1, 1), log_scale_ref[0], jnp.float32))
    offset = jnp.full((1, 1), bias_ref[0], jnp.float32)
    everything = keys.at[pl.ds(0, n_all - 1)]

    def compute(e):
        _, _, _, bi, zz = place_of(e)
        arrived(slot(bi, zz, 1 - c), None)
        pair = bi * n_z + zz
        start = pair * 2 * rows
        block = buf[pl.ds(pl.multiple_of(start, 2 * rows), 2 * rows), :]
        scores = lax.dot_general(
            buf[own, :], block, (((1,), (1,)), ((), ())), preferred_element_type=jnp.float32
        )
        lanes = lax.broadcasted_iota(jnp.int32, (rows, 128), 1)
        here = lax.broadcasted_iota(jnp.int32, (rows, 128), 0) + me * rows
        weights = []
        for u in range(2 * rows // 128):
            side, at = u * 128 // rows, u * 128 % rows
            columns = lanes + (start + u * 128)
            named = jnp.zeros((rows, 128), jnp.float32)
            for k in range(most):
                named += jnp.where(wanted[k] == columns, 1.0, 0.0)
            for k in range(most):
                key = keys[pair * 2 + side, k : k + 1, at : at + 128]
                named += jnp.where(key == here, 1.0, 0.0)
            power = jnp.exp(offset + scale * scores[:, u * 128 : (u + 1) * 128])
            gain = jnp.where(jnp.logical_and(zz == z, c == side), 2.0, 0.0)
            negative = jnp.where(columns == here, 0.0, gain * power)
            weights.append(((negative - named) / (1.0 + power)).astype(jnp.bfloat16))
        weight = jnp.concatenate(weights, axis=1)
        acc[...] += jnp.dot(weight, block, preferred_element_type=jnp.float32)

    @pl.loop(0, events + n_blk)
    def _(e):
        t, m, d, bi, zz = place_of(e)
        valid = jnp.logical_and(t >= 0, t < n_z)

        for step, k in ((1, 1), (-1, 0)):
            origin = z + step * (t + 1)

            @pl.when(jnp.logical_and(m == 0, jnp.logical_and(origin >= 0, origin < n_z)))
            def _():
                f = slot(i, origin, c)
                arrived(f, None)

                @pl.when(jnp.logical_and(z - step >= 0, z - step < n_z))
                def _():
                    along_z(origin, -step, k).start()

                to_right(f, None, origin).start()
                to_left(f, None, origin).start()
                to_sib(f, origin).start()

        f = slot(bi, zz, c)
        passing = jnp.logical_and(valid, jnp.logical_and(m > 0, m < n_blk - 1))

        @pl.when(passing)
        def _():
            arrived(f, None)

        for parity, send in ((1, to_right), (0, to_left)):
            mine = jnp.logical_and(passing, m % 2 == parity)

            @pl.when(jnp.logical_and(jnp.logical_and(mine, halves(zz)), d == far - 1))
            def _():
                send(f, 1 - parity, m * n_z + zz).start()

            if far > 2:
                @pl.when(jnp.logical_and(mine, d < far - 1))
                def _():
                    send(f, None, m * n_z + zz).start()

        @pl.when(jnp.logical_and(passing, m > 0))
        def _():
            to_sib(f, m * n_z + zz).start()

        for step, k in ((1, 1), (-1, 0)):
            origin = z + step * t
            here = jnp.logical_and(origin >= 0, origin < n_z)
            here = jnp.logical_and(here, jnp.logical_and(m == n_blk - 1, valid))
            if step < 0:
                here = jnp.logical_and(here, t > 0)

            @pl.when(here)
            def _():
                g = slot(far_blk, origin, c)

                @pl.when(halves(origin))
                def _():
                    arrived(g, 0)
                    arrived(g, 1)

                @pl.when(jnp.logical_not(halves(origin)))
                def _():
                    arrived(g, None)

                @pl.when(t + 1 <= reach(z - step))
                def _():
                    far_along_z(origin, -step, k).start()

                @pl.when(jnp.logical_and(t == 0, 1 <= reach(z + step)))
                def _():
                    far_along_z(origin, step, 1 - k).start()

                to_sib(g, (n_blk - 1) * n_z + origin).start()

        @pl.when(e == 1)
        def _():
            key_copy(everything, everything, lax.rem(me + 1, n_all)).wait()

        before = place_of(e - 1 + n_blk)[0] - 1

        @pl.when(jnp.logical_and(e > 0, jnp.logical_and(before >= 0, before < n_z)))
        def _():
            compute(e - 1)

    compute(events + n_blk - 1)

    t_acc = scale * acc[...]
    x = x_ref[...].astype(jnp.float32)
    inv = lax.rsqrt(jnp.mean(x * x, axis=1, keepdims=True) + 1e-06)
    inner = jnp.sum(x * t_acc, axis=1, keepdims=True)
    o_ref[...] = (root * inv * (t_acc - x * (inv * inv * inner / width))).astype(o_ref.dtype)

    @pl.loop(0, n_z)
    def _(zz):
        @pl.when(jnp.logical_and(zz <= z, z < n_z - 1))
        def _():
            along_z(zz, 1, 0).wait_send()

        @pl.when(jnp.logical_and(zz >= z, z > 0))
        def _():
            along_z(zz, -1, 1).wait_send()

        @pl.when(jnp.logical_and(zz <= z, z + 1 - zz <= reach(z + 1)))
        def _():
            far_along_z(zz, 1, 0).wait_send()

        @pl.when(jnp.logical_and(zz >= z, zz - z + 1 <= reach(z - 1)))
        def _():
            far_along_z(zz, -1, 1).wait_send()

    @pl.loop(0, events)
    def _(e):
        m, zz = e // n_z, e % n_z
        to_sib(me, e).wait_send()

        @pl.when(m == 0)
        def _():
            to_right(me, None, e).wait_send()
            to_left(me, None, e).wait_send()

        passing = jnp.logical_and(m > 0, m < n_blk - 1)
        for parity, send in ((1, to_right), (0, to_left)):
            mine = jnp.logical_and(passing, m % 2 == parity)

            @pl.when(jnp.logical_and(jnp.logical_and(mine, halves(zz)), (m + 1) // 2 == far - 1))
            def _():
                send(me, 0, e).wait_send()

            if far > 2:
                @pl.when(jnp.logical_and(mine, (m + 1) // 2 < far - 1))
                def _():
                    send(me, None, e).wait_send()


def body(n_blk, n_dp, embed, log_scale, bias, partner_count, partner_owner, partner_row):
    rows, width = embed.shape
    most = partner_owner.shape[1]
    n_all = n_blk * n_dp
    events = n_all // 2
    live = jnp.arange(most, dtype=jnp.int32)[:, None] < partner_count[None, :]
    theirs = jnp.where(live, partner_owner.T * rows + partner_row.T, -1).reshape(1, most, rows)
    vmem = pl.BlockSpec(memory_space=pltpu.VMEM)
    smem = pl.BlockSpec(memory_space=pltpu.SMEM)
    return pl.pallas_call(
        functools.partial(kernel, n_blk, n_dp),
        out_shape=jax.ShapeDtypeStruct((rows, width), embed.dtype),
        in_specs=[smem, smem, vmem, vmem],
        out_specs=vmem,
        scratch_shapes=[
            pltpu.VMEM((n_all * rows, width), jnp.bfloat16),
            pltpu.VMEM((n_all, most, rows), jnp.int32),
            pltpu.VMEM((rows, width), jnp.float32),
            pltpu.VMEM((most, rows, 128), jnp.int32),
            pltpu.SemaphoreType.DMA((n_dp // 2, 4)),
            pltpu.SemaphoreType.DMA((events,)),
            pltpu.SemaphoreType.DMA((events,)),
            pltpu.SemaphoreType.DMA((events,)),
            pltpu.SemaphoreType.DMA((n_all, 2)),
            pltpu.SemaphoreType.DMA,
            pltpu.SemaphoreType.DMA,
        ],
        compiler_params=pltpu.CompilerParams(
            collective_id=0, has_side_effects=True, vmem_limit_bytes=60 * 1024 * 1024
        ),
    )(log_scale, bias, embed, theirs)


def solution(mesh):
    return jax.shard_map(
        functools.partial(body, mesh.shape["blk"], mesh.shape["dp"]),
        mesh=mesh,
        in_specs=(
            P(("blk", "dp"), None),
            P(),
            P(),
            P(("blk", "dp")),
            P(("blk", "dp"), None),
            P(("blk", "dp"), None),
        ),
        out_specs=P(("blk", "dp"), None),
        check_vma=False,
    )
```

```python
import functools
import math

import jax
import jax.numpy as jnp
from jax import lax
from jax.experimental import pallas as pl
from jax.experimental.pallas import tpu as pltpu
from jax.sharding import PartitionSpec as P

MESH = pl.DeviceIdType.MESH


def lookup(table, index):
    value = jnp.int32(table[0])
    for k in range(1, len(table)):
        value = jnp.where(index == k, jnp.int32(table[k]), value)
    return value


def kernel(
    n_blk, n_dp, log_scale_ref, bias_ref, x_ref, theirs_ref, o_ref,
    buf, keys, acc, wanted, z_sem, right_sem, left_sem, sib_sem, recv_sem, key_send, key_recv,
):
    rows, width = x_ref.shape
    most = theirs_ref.shape[1]
    half = rows // 2
    n_all = n_blk * n_dp
    n_z = n_dp // 2
    far = n_blk // 2
    events = n_blk * n_z
    i, j = lax.axis_index("blk"), lax.axis_index("dp")
    z, c = j // 2, j % 2
    me = i * n_dp + j

    ring = [p ^ (p >> 1) for p in range(n_blk)]
    place = [ring.index(k) for k in range(n_blk)]
    pos = lookup(place, i)
    blk_at = lambda p: lookup(ring, lax.rem(p + n_blk, n_blk))
    right, left = blk_at(pos + 1), blk_at(pos - 1)
    order = []
    for a in range(n_z):
        order += sorted(range(n_z), key=lambda b: (abs(b - a), b))
    z_at = lambda t: lookup(order, z * n_z + t)
    slot = lambda bi, zz, cc: (bi * n_z + zz) * 2 + cc

    def copy(f, h, device, send, recv):
        if h is None:
            span = pl.ds(pl.multiple_of(f * rows, rows), rows)
        else:
            span = pl.ds(pl.multiple_of(f * rows + h * half, half), half)
        return pltpu.make_async_remote_copy(
            src_ref=buf.at[span], dst_ref=buf.at[span], send_sem=send, recv_sem=recv,
            device_id=device, device_id_type=MESH,
        )

    def to_right(f, h, e):
        return copy(f, h, (right, j), right_sem.at[e], recv_sem.at[f, h or 0])

    def to_left(f, h, e):
        return copy(f, h, (left, j), left_sem.at[e], recv_sem.at[f, h or 0])

    def to_sib(f, e):
        return copy(f, None, (i, z * 2 + 1 - c), sib_sem.at[e], recv_sem.at[f, 0])

    def along_z(zz, step, k):
        f = slot(i, zz, c)
        return copy(f, None, (i, (z + step) * 2 + c), z_sem.at[zz, k], recv_sem.at[f, 0])

    far_blk = blk_at(pos + far)

    def far_along_z(zz, step, k):
        f = slot(far_blk, zz, c)
        return copy(f, None, (i, (z + step) * 2 + c), z_sem.at[zz, 2 + k], recv_sem.at[f, 0])

    def reach(zz):
        return jnp.where(jnp.logical_and(zz >= 0, zz < n_z), 1, 0)

    def halves(zz):
        return jnp.logical_or(zz == z, jnp.maximum(zz - z, z - zz) > reach(z))

    def arrived(f, h):
        copy(f, h, (right, j), right_sem.at[0], recv_sem.at[f, h or 0]).wait_recv()

    def place_of(e):
        t, m = e // n_blk, e % n_blk
        t = jnp.where(m == n_blk - 1, t - 1, t)
        d = (m + 1) // 2
        return t, m, d, blk_at(jnp.where(m % 2 == 1, pos - d, pos + d)), z_at(t)

    barrier = pltpu.get_barrier_semaphore()

    @pl.loop(1, n_all)
    def _(k):
        f = lax.rem(me + k, n_all)
        pl.semaphore_signal(barrier, 1, device_id=(f // n_dp, f % n_dp), device_id_type=MESH)

    root = 1.0 / math.sqrt(width)
    x = x_ref[...].astype(jnp.float32)
    inv = lax.rsqrt(jnp.mean(x * x, axis=1, keepdims=True) + 1e-06)
    own = pl.ds(pl.multiple_of(me * rows, rows), rows)
    buf[own, :] = (x * inv * root).astype(jnp.bfloat16)
    keys[pl.ds(me, 1)] = theirs_ref[...]
    pl.semaphore_wait(barrier, n_all - 1)

    to_right(me, None, z).start()
    to_left(me, None, z).start()

    @pl.when(z < n_z - 1)
    def _():
        along_z(z, 1, 0).start()

    @pl.when(z > 0)
    def _():
        along_z(z, -1, 1).start()

    to_sib(me, z).start()

    def key_copy(src, dst, f):
        return pltpu.make_async_remote_copy(
            src_ref=src, dst_ref=dst, send_sem=key_send, recv_sem=key_recv,
            device_id=(f // n_dp, f % n_dp), device_id_type=MESH,
        )

    @pl.loop(1, n_all)
    def _(k):
        f = lax.rem(me + k, n_all)
        key_copy(theirs_ref, keys.at[pl.ds(me, 1)], f).start()

    acc[...] = jnp.zeros_like(acc)
    for k in range(most):
        wanted[k] = jnp.broadcast_to(theirs_ref[0, k : k + 1, :], (128, rows)).T
    scale = jnp.exp(jnp.full((1, 1), log_scale_ref[0], jnp.float32))
    offset = jnp.full((1, 1), bias_ref[0], jnp.float32)
    everything = keys.at[pl.ds(0, n_all - 1)]

    def compute(e):
        _, _, _, bi, zz = place_of(e)
        arrived(slot(bi, zz, 1 - c), None)
        pair = bi * n_z + zz
        start = pair * 2 * rows
        block = buf[pl.ds(pl.multiple_of(start, 2 * rows), 2 * rows), :]
        scores = lax.dot_general(
            buf[own, :], block, (((1,), (1,)), ((), ())), preferred_element_type=jnp.float32
        )
        lanes = lax.broadcasted_iota(jnp.int32, (rows, 128), 1)
        here = lax.broadcasted_iota(jnp.int32, (rows, 128), 0) + me * rows
        weights = []
        for u in range(2 * rows // 128):
            side, at = u * 128 // rows, u * 128 % rows
            columns = lanes + (start + u * 128)
            named = jnp.zeros((rows, 128), jnp.float32)
            for k in range(most):
                named += jnp.where(wanted[k] == columns, 1.0, 0.0)
            for k in range(most):
                key = keys[pair * 2 + side, k : k + 1, at : at + 128]
                named += jnp.where(key == here, 1.0, 0.0)
            power = jnp.exp(offset + scale * scores[:, u * 128 : (u + 1) * 128])
            gain = jnp.where(jnp.logical_and(zz == z, c == side), 2.0, 0.0)
            negative = jnp.where(columns == here, 0.0, gain * power)
            weights.append(((negative - named) / (1.0 + power)).astype(jnp.bfloat16))
        weight = jnp.concatenate(weights, axis=1)
        acc[...] += jnp.dot(weight, block, preferred_element_type=jnp.float32)

    @pl.loop(0, events + n_blk)
    def _(e):
        t, m, d, bi, zz = place_of(e)
        valid = jnp.logical_and(t >= 0, t < n_z)

        for step, k in ((1, 1), (-1, 0)):
            origin = z + step * (t + 1)

            @pl.when(jnp.logical_and(m == 0, jnp.logical_and(origin >= 0, origin < n_z)))
            def _():
                f = slot(i, origin, c)
                arrived(f, None)

                @pl.when(jnp.logical_and(z - step >= 0, z - step < n_z))
                def _():
                    along_z(origin, -step, k).start()

                to_right(f, None, origin).start()
                to_left(f, None, origin).start()
                to_sib(f, origin).start()

        passing = jnp.logical_and(valid, jnp.logical_and(m % 2 == 1, m < n_blk - 1))
        for parity, send in ((1, to_right), (0, to_left)):
            f = slot(blk_at(pos - d if parity else pos + d), zz, c)
            index = (2 * d - parity) * n_z + zz

            @pl.when(passing)
            def _():
                arrived(f, None)

            @pl.when(jnp.logical_and(jnp.logical_and(passing, halves(zz)), d == far - 1))
            def _():
                send(f, 1 - parity, index).start()

            if far > 2:
                @pl.when(jnp.logical_and(passing, d < far - 1))
                def _():
                    send(f, None, index).start()

            @pl.when(passing)
            def _():
                to_sib(f, index).start()

        for step, k in ((1, 1), (-1, 0)):
            origin = z + step * t
            here = jnp.logical_and(origin >= 0, origin < n_z)
            here = jnp.logical_and(here, jnp.logical_and(m == n_blk - 1, valid))
            if step < 0:
                here = jnp.logical_and(here, t > 0)

            @pl.when(here)
            def _():
                g = slot(far_blk, origin, c)

                @pl.when(halves(origin))
                def _():
                    arrived(g, 0)
                    arrived(g, 1)

                @pl.when(jnp.logical_not(halves(origin)))
                def _():
                    arrived(g, None)

                @pl.when(t + 1 <= reach(z - step))
                def _():
                    far_along_z(origin, -step, k).start()

                @pl.when(jnp.logical_and(t == 0, 1 <= reach(z + step)))
                def _():
                    far_along_z(origin, step, 1 - k).start()

                to_sib(g, (n_blk - 1) * n_z + origin).start()

        @pl.when(e == 1)
        def _():
            key_copy(everything, everything, lax.rem(me + 1, n_all)).wait()

        before = place_of(e - 1 + n_blk)[0] - 1

        @pl.when(jnp.logical_and(e > 0, jnp.logical_and(before >= 0, before < n_z)))
        def _():
            compute(e - 1)

    compute(events + n_blk - 1)

    t_acc = scale * acc[...]
    x = x_ref[...].astype(jnp.float32)
    inv = lax.rsqrt(jnp.mean(x * x, axis=1, keepdims=True) + 1e-06)
    inner = jnp.sum(x * t_acc, axis=1, keepdims=True)
    o_ref[...] = (root * inv * (t_acc - x * (inv * inv * inner / width))).astype(o_ref.dtype)

    @pl.loop(0, n_z)
    def _(zz):
        @pl.when(jnp.logical_and(zz <= z, z < n_z - 1))
        def _():
            along_z(zz, 1, 0).wait_send()

        @pl.when(jnp.logical_and(zz >= z, z > 0))
        def _():
            along_z(zz, -1, 1).wait_send()

        @pl.when(jnp.logical_and(zz <= z, z + 1 - zz <= reach(z + 1)))
        def _():
            far_along_z(zz, 1, 0).wait_send()

        @pl.when(jnp.logical_and(zz >= z, zz - z + 1 <= reach(z - 1)))
        def _():
            far_along_z(zz, -1, 1).wait_send()

    @pl.loop(0, events)
    def _(e):
        m, zz = e // n_z, e % n_z
        to_sib(me, e).wait_send()

        @pl.when(m == 0)
        def _():
            to_right(me, None, e).wait_send()
            to_left(me, None, e).wait_send()

        passing = jnp.logical_and(m > 0, m < n_blk - 1)
        for parity, send in ((1, to_right), (0, to_left)):
            mine = jnp.logical_and(passing, m % 2 == parity)

            @pl.when(jnp.logical_and(jnp.logical_and(mine, halves(zz)), (m + 1) // 2 == far - 1))
            def _():
                send(me, 0, e).wait_send()

            if far > 2:
                @pl.when(jnp.logical_and(mine, (m + 1) // 2 < far - 1))
                def _():
                    send(me, None, e).wait_send()


def body(n_blk, n_dp, embed, log_scale, bias, partner_count, partner_owner, partner_row):
    rows, width = embed.shape
    most = partner_owner.shape[1]
    n_all = n_blk * n_dp
    events = n_all // 2
    live = jnp.arange(most, dtype=jnp.int32)[:, None] < partner_count[None, :]
    theirs = jnp.where(live, partner_owner.T * rows + partner_row.T, -1).reshape(1, most, rows)
    vmem = pl.BlockSpec(memory_space=pltpu.VMEM)
    smem = pl.BlockSpec(memory_space=pltpu.SMEM)
    return pl.pallas_call(
        functools.partial(kernel, n_blk, n_dp),
        out_shape=jax.ShapeDtypeStruct((rows, width), embed.dtype),
        in_specs=[smem, smem, vmem, vmem],
        out_specs=vmem,
        scratch_shapes=[
            pltpu.VMEM((n_all * rows, width), jnp.bfloat16),
            pltpu.VMEM((n_all, most, rows), jnp.int32),
            pltpu.VMEM((rows, width), jnp.float32),
            pltpu.VMEM((most, rows, 128), jnp.int32),
            pltpu.SemaphoreType.DMA((n_dp // 2, 4)),
            pltpu.SemaphoreType.DMA((events,)),
            pltpu.SemaphoreType.DMA((events,)),
            pltpu.SemaphoreType.DMA((events,)),
            pltpu.SemaphoreType.DMA((n_all, 2)),
            pltpu.SemaphoreType.DMA,
            pltpu.SemaphoreType.DMA,
        ],
        compiler_params=pltpu.CompilerParams(
            collective_id=0, has_side_effects=True, vmem_limit_bytes=60 * 1024 * 1024
        ),
    )(log_scale, bias, embed, theirs)


def solution(mesh):
    return jax.shard_map(
        functools.partial(body, mesh.shape["blk"], mesh.shape["dp"]),
        mesh=mesh,
        in_specs=(
            P(("blk", "dp"), None),
            P(),
            P(),
            P(("blk", "dp")),
            P(("blk", "dp"), None),
            P(("blk", "dp"), None),
        ),
        out_specs=P(("blk", "dp"), None),
        check_vma=False,
    )
```
